768 devices in a mesh: section: 8 (over y), dp: 8 (over z_hi, core), mp: 12 (over x, z_lo).
Axes of the slice: x: 4, y: 8, z: 12 (z_hi: 4, z_lo: 3; z = z_hi * 3 + z_lo), core: 2. Of those that a mesh axis runs over, the one named last changes fastest.
Arguments:
- activations: bfloat16 [6144, 27648], P(('dp', 'section'), 'mp'), may hold values from -6 to 6
- weight: bfloat16 [27648, 5120], P('mp', 'section'), may hold values from -0.0390625 to 0.0390625
- readout: bfloat16 [6144, 5120], P('dp', 'section'), may hold values from -0.02734375 to 0.02734375
- logp_rest: float32 [6144], P('dp'), may hold values from -1.2 to 1.2
- old_logp: float32 [6144], P('dp'), may hold values from -1.2 to 1.2
- ref_logp: float32 [6144], P('dp'), may hold values from -4 to 4
- lengths: int32 [16], replicated, may hold values from 1 to 384, as said below
- group_ids: int32 [16], replicated, may hold values from 0 to 7, as said below
- rewards: float32 [16], replicated, may hold values from -6 to 6
- first_moment: float32 [12, 2304, 5120], P('mp', 'dp', 'section'), may hold values from -0.0006 to 0.0006
- second_moment: float32 [12, 2304, 5120], P('mp', 'dp', 'section'), may hold values from 1e-10 to 1e-05
Outputs:
- new_weight: bfloat16 [27648, 5120], P('mp', 'section')
- new_first: float32 [12, 2304, 5120], P('mp', 'dp', 'section')
- new_second: float32 [12, 2304, 5120], P('mp', 'dp', 'section')
The draws below stay inside these ranges and needn't reach their ends.
Inputs may be any that keep to these rules, and one draw needn't show every extreme that they name: `lengths`: every response has at least one live token, and some response has all 384 slots live. `group_ids`: each group id names exactly 2 responses.
All inputs are finite; a program needn't handle non-finite values.
Results may differ from the reference program's by a relative error of at most 0.015.
Values may be sent and summed in bfloat16 or wider, within the bound.
No kernel may reach another device: no remote copies, remote signals or barrier semaphores. Data moves between devices by JAX's collectives and lax.ppermute only.
A program may use at most 64 MiB of HBM per device.

```python
import math
import jax
import jax.numpy as jnp
from jax import lax

D = 5120
FF = 27648
RESP_LEN = 384
GROUP = 2
TOK_REP = 768
TOKENS = 6144
RESP = 16
N_DP = 8
N_MP = 12


def draw_lengths(key, part):
    first_key, second_key = jax.random.split(jax.random.fold_in(key, 11))
    drawn = jax.random.randint(first_key, (RESP,), 1, RESP_LEN + 1)
    longest = jax.random.randint(second_key, (), 0, RESP)
    return jnp.where(jnp.arange(RESP) == longest, RESP_LEN, drawn).astype(jnp.int32)


def draw_group_ids(key, part):
    shuffled = jax.random.permutation(jax.random.fold_in(key, 23), RESP)
    return (shuffled // GROUP).astype(jnp.int32)


def levels(stream_key, extent, cuts, least, top_value):
    factor_of = 1.0
    for dim, parts in cuts:
        draws = jax.random.uniform(jax.random.fold_in(jax.random.fold_in(stream_key, 6), dim), (parts,), jnp.float32, least / len(cuts), top_value / len(cuts))
        factor_of = factor_of * jnp.repeat(jnp.exp(draws), extent[dim] // parts).reshape((-1,) + (1,) * (len(extent) - 1 - dim))
    return factor_of


def normal_values(own_key, dims, spread, reach, pieces=(), held_as=jnp.bfloat16):
    values = spread * jax.random.normal(own_key, dims, jnp.float32)
    if pieces:
        values = values * levels(own_key, dims, pieces, -0.22, 0.18)
    return jnp.clip(values, -reach, reach).astype(held_as)


def setup_inputs(seed: int = 0) -> dict:
    keys = jax.random.split(jax.random.key(seed), 12)
    activations = normal_values(keys[0], (TOKENS, FF), 1.0, 6.0, ((0, 64), (1, 12)))
    weight = normal_values(keys[1], (FF, D), FF ** -0.5, 0.0390625, ((0, 12), (1, 8)))
    readout = normal_values(keys[2], (TOKENS, D), (D * 11) ** -0.5, 0.02734375, ((0, 8), (1, 8)))
    logp_rest = normal_values(keys[3], (TOKENS,), 0.2, 1.2, ((0, 8),), jnp.float32)
    old_logp = normal_values(keys[4], (TOKENS,), 0.2, 1.2, ((0, 8),), jnp.float32)
    ref_logp = normal_values(keys[5], (TOKENS,), 0.8, 4.0, ((0, 8),), jnp.float32)
    lengths = draw_lengths(jax.random.fold_in(keys[11], 71), 0)
    group_ids = draw_group_ids(jax.random.fold_in(keys[11], 71), 0)
    rewards = normal_values(keys[8], (RESP,), 1.5, 6.0, (), jnp.float32)
    first_moment = normal_values(keys[9], (N_MP, FF // N_MP, D), 0.0001, 0.0006, ((0, 12), (1, 8), (2, 8)), jnp.float32)
    second_moment = jnp.clip(jnp.exp(math.log(9.999999747378752e-06) - 11.512925 * jax.random.uniform(keys[10], (N_MP, FF // N_MP, D), jnp.float32) ** levels(keys[10], (N_MP, FF // N_MP, D), ((0, 12), (1, 8), (2, 8)), -0.2, 0.2)), 1.000000013351432e-10, 9.999999747378752e-06)
    return dict(activations=activations, weight=weight, readout=readout, logp_rest=logp_rest, old_logp=old_logp, ref_logp=ref_logp, lengths=lengths, group_ids=group_ids, rewards=rewards, first_moment=first_moment, second_moment=second_moment)


clip_eps = 0.2
kl_coef = 0.1
beta_one = 0.9
beta_two = 0.95
adam_eps = 1e-08
learn_rate = 0.0003
weight_decay = 0.1
first_correct = 1.0 - 0.9 ** 10
second_correct = 1.0 - 0.95 ** 10

def token_terms(lengths, group_ids, rewards, positions, resp_len):
    total_resp = rewards.shape[0]
    members = (group_ids[:, None] == group_ids[None, :]).astype(jnp.float32)
    group_size = lax.optimization_barrier(jnp.sum(members, axis=1))
    group_mean = lax.optimization_barrier(jnp.sum(members * rewards[None, :], axis=1)) / group_size
    deviation = rewards[None, :] - group_mean[:, None]
    group_spread = jnp.sqrt(lax.optimization_barrier(jnp.sum(members * deviation * deviation, axis=1)) / group_size)
    advantage = (rewards - group_mean) / jnp.maximum(group_spread, 1.0)
    response = positions // resp_len
    slot_index = (positions % resp_len).astype(jnp.float32)
    picker = (response[:, None] == jnp.arange(total_resp, dtype=jnp.int32)[None, :]).astype(jnp.float32)
    adv_token = lax.optimization_barrier(jnp.sum(picker * advantage[None, :], axis=1))
    len_token = lax.optimization_barrier(jnp.sum(picker * lengths.astype(jnp.float32)[None, :], axis=1))
    token_weight = jnp.where(slot_index < len_token, 1.0 / (len_token * total_resp), 0.0)
    return (adv_token, token_weight)

def token_loss(new_logp, old_logp, ref_logp, adv_token, token_weight):
    ratio = jnp.exp(new_logp - old_logp)
    surrogate = jnp.minimum(ratio * adv_token, jnp.clip(ratio, 1.0 - clip_eps, 1.0 + clip_eps) * adv_token)
    gap = ref_logp - new_logp
    kl_term = jnp.exp(gap) - gap - 1.0
    return jnp.sum(token_weight * (kl_coef * kl_term - surrogate))

def token_coeff(new_logp, old_logp, ref_logp, adv_token, token_weight):

    def loss_of(values):
        return token_loss(values, old_logp, ref_logp, adv_token, token_weight)
    _, pullback = jax.vjp(loss_of, new_logp)
    return pullback(jnp.float32(1.0))[0]

def adam_rows(weight_rows, first_rows, second_rows, gradient):
    new_first = beta_one * first_rows + (1.0 - beta_one) * gradient
    new_second = beta_two * second_rows + (1.0 - beta_two) * gradient * gradient
    current = weight_rows.astype(jnp.float32)
    update = new_first / first_correct / (jnp.sqrt(new_second / second_correct) + adam_eps) + weight_decay * current
    return ((current - learn_rate * update).astype(jnp.bfloat16), new_first, new_second)

def reference(activations, weight, readout, logp_rest, old_logp, ref_logp, lengths, group_ids, rewards, first_moment, second_moment):
    layer_out = jnp.dot(activations, weight, preferred_element_type=jnp.float32)
    score = lax.optimization_barrier(jnp.sum(layer_out * readout.astype(jnp.float32), axis=1))
    new_logp = logp_rest + score
    positions = jnp.arange(TOKENS, dtype=jnp.int32)
    adv_token, token_weight = token_terms(lengths, group_ids, rewards, positions, RESP_LEN)
    coeff = token_coeff(new_logp, old_logp, ref_logp, adv_token, token_weight)
    weighted = (coeff[:, None] * readout.astype(jnp.float32)).astype(jnp.bfloat16)
    act_blocks = activations.reshape(N_DP, TOK_REP, FF)
    weighted_blocks = weighted.reshape(N_DP, TOK_REP, D)

    def add_replica(total, pair):
        part = lax.dot_general(pair[0], pair[1], (((0,), (0,)), ((), ())), preferred_element_type=jnp.float32)
        return (total + part.astype(jnp.bfloat16).astype(jnp.float32), None)
    gradient, _ = lax.scan(add_replica, jnp.zeros((FF, D), jnp.float32), (act_blocks, weighted_blocks))
    first_flat = first_moment.reshape(FF, D)
    second_flat = second_moment.reshape(FF, D)
    new_weight, new_first, new_second = adam_rows(weight, first_flat, second_flat, gradient)
    return (new_weight, new_first.reshape(N_MP, FF // N_MP, D), new_second.reshape(N_MP, FF // N_MP, D))
```

```python
import jax
import jax.numpy as jnp
from jax import lax
from jax.sharding import PartitionSpec as P

RESP_LEN = 384


clip_eps = 0.2
kl_coef = 0.1
beta_one = 0.9
beta_two = 0.95
adam_eps = 1e-08
learn_rate = 0.0003
weight_decay = 0.1
first_correct = 1.0 - 0.9**10
second_correct = 1.0 - 0.95**10


def token_terms(lengths, group_ids, rewards, positions, resp_len):
    total_resp = rewards.shape[0]
    members = (group_ids[:, None] == group_ids[None, :]).astype(jnp.float32)
    group_size = jnp.sum(members, axis=1)
    group_mean = jnp.sum(members * rewards[None, :], axis=1) / group_size
    deviation = rewards[None, :] - group_mean[:, None]
    group_spread = jnp.sqrt(jnp.sum(members * deviation * deviation, axis=1) / group_size)
    advantage = (rewards - group_mean) / jnp.maximum(group_spread, 1.0)
    response = positions // resp_len
    slot_index = (positions % resp_len).astype(jnp.float32)
    picker = (response[:, None] == jnp.arange(total_resp, dtype=jnp.int32)[None, :]).astype(
        jnp.float32
    )
    adv_token = jnp.sum(picker * advantage[None, :], axis=1)
    len_token = jnp.sum(picker * lengths.astype(jnp.float32)[None, :], axis=1)
    token_weight = jnp.where(slot_index < len_token, 1.0 / (len_token * total_resp), 0.0)
    return (adv_token, token_weight)


def token_loss(new_logp, old_logp, ref_logp, adv_token, token_weight):
    ratio = jnp.exp(new_logp - old_logp)
    surrogate = jnp.minimum(
        ratio * adv_token, jnp.clip(ratio, 1.0 - clip_eps, 1.0 + clip_eps) * adv_token
    )
    gap = ref_logp - new_logp
    kl_term = jnp.exp(gap) - gap - 1.0
    return jnp.sum(token_weight * (kl_coef * kl_term - surrogate))


def token_coeff(new_logp, old_logp, ref_logp, adv_token, token_weight):

    def loss_of(values):
        return token_loss(values, old_logp, ref_logp, adv_token, token_weight)

    _, pullback = jax.vjp(loss_of, new_logp)
    return pullback(jnp.float32(1.0))[0]


def adam_rows(weight_rows, first_rows, second_rows, gradient):
    new_first = beta_one * first_rows + (1.0 - beta_one) * gradient
    new_second = beta_two * second_rows + (1.0 - beta_two) * gradient * gradient
    current = weight_rows.astype(jnp.float32)
    update = (
        new_first / first_correct / (jnp.sqrt(new_second / second_correct) + adam_eps)
        + weight_decay * current
    )
    return ((current - learn_rate * update).astype(jnp.bfloat16), new_first, new_second)


def contract_rows(left, right):
    return lax.dot_general(
        left, right, (((0,), (0,)), ((), ())), preferred_element_type=jnp.float32
    )


N_SEC = 8
N_Z = 4
N_CORE = 2
N_X = 4
N_ZLO = 3


def along_section(value, step):
    return lax.ppermute(value, "section", [(i, (i + step) % N_SEC) for i in range(N_SEC)])


def along_z(value, step):
    pairs = [
        (N_CORE * z + c, N_CORE * ((z + step) % N_Z) + c) for z in range(N_Z) for c in range(N_CORE)
    ]
    return lax.ppermute(value, "dp", pairs)


def to_other_core(value):
    return lax.ppermute(value, "dp", [(i, i ^ 1) for i in range(N_Z * N_CORE)])


def turned(value, blocks):
    twice = jnp.concatenate([value, value], axis=0)
    return lax.dynamic_slice_in_dim(
        twice, blocks * (value.shape[0] // N_SEC), value.shape[0], 0
    )


def reduce_scores(share):
    copies = jnp.broadcast_to(share[None, :], (N_SEC * N_X * N_ZLO, share.shape[0]))
    shares = lax.all_to_all(copies, ("section", "mp"), 0, 0)
    return jnp.sum(shares, axis=0)


def on_device(
    activations,
    weight,
    readout,
    logp_rest,
    old_logp,
    ref_logp,
    lengths,
    group_ids,
    rewards,
    first_moment,
    second_moment,
):
    tok_block = activations.shape[0]
    tok_rep = tok_block * N_SEC
    section = lax.axis_index("section")
    dp = lax.axis_index("dp")
    core = dp % N_CORE
    z_hi = dp // N_CORE

    def own_first(value):
        return turned(value, section)

    readout = own_first(readout)

    def score_of(chunk, first_row):
        rows = lax.slice_in_dim(readout, first_row, first_row + chunk.shape[0], axis=0)
        product = jnp.dot(chunk, weight, preferred_element_type=jnp.float32)
        return jnp.sum(product * rows.astype(jnp.float32), axis=1)

    chunks = [None] * N_SEC
    chunks[0] = activations
    below = above = activations
    for step in range(1, N_SEC // 2):
        below = along_section(below, 1)
        above = along_section(above, -1)
        chunks[N_SEC - step] = below
        chunks[step] = above
    half = tok_block // 2
    chunks[N_SEC // 2] = jnp.concatenate(
        [along_section(below[:half], 1), along_section(above[half:], -1)]
    )
    scores = [score_of(chunks[j], j * tok_block) for j in range(N_SEC)]
    gathered = jnp.concatenate(chunks)
    share = turned(jnp.concatenate(scores), (N_SEC - section) % N_SEC)
    score = own_first(reduce_scores(share))

    new_logp = own_first(logp_rest) + score
    slots = jnp.arange(tok_rep, dtype=jnp.int32)
    positions = dp * tok_rep + (slots + section * tok_block) % tok_rep
    adv_token, token_weight = token_terms(lengths, group_ids, rewards, positions, RESP_LEN)
    coeff = token_coeff(
        new_logp, own_first(old_logp), own_first(ref_logp), adv_token, token_weight
    )
    weighted = (coeff[:, None] * readout.astype(jnp.float32)).astype(jnp.bfloat16)
    shard_rows = first_moment.shape[1]
    part = contract_rows(gathered, weighted).astype(jnp.bfloat16)

    def part_rows(step, which_core):
        shard = N_CORE * ((z_hi + step) % N_Z) + which_core
        return lax.dynamic_slice_in_dim(part, shard * shard_rows, shard_rows, 0)

    mine = {}
    for step in (3, 1, 2, 0):
        kept = part_rows(step, core).astype(jnp.float32)
        mine[step] = kept + to_other_core(part_rows(step, 1 - core)).astype(jnp.float32)
    low = shard_rows // 2

    def sent(value):
        return value.astype(jnp.bfloat16)

    up = along_z(sent(mine[3][:low]), 1).astype(jnp.float32)
    down = along_z(sent(mine[1][low:]), -1).astype(jnp.float32)
    up = along_z(sent(up + mine[2][:low]), 1).astype(jnp.float32)
    down = along_z(sent(down + mine[2][low:]), -1).astype(jnp.float32)
    up = along_z(sent(up + mine[1][:low]), 1).astype(jnp.float32)
    down = along_z(sent(down + mine[3][low:]), -1).astype(jnp.float32)
    gradient = jnp.concatenate([up + mine[0][:low], down + mine[0][low:]])

    weight_rows = lax.dynamic_slice_in_dim(weight, dp * shard_rows, shard_rows, 0)
    updated, new_first, new_second = adam_rows(
        weight_rows, first_moment[0], second_moment[0], gradient
    )

    from_below = along_z(updated, 1)
    from_above = along_z(updated, -1)
    opposite = jnp.concatenate([along_z(from_below[:low], 1), along_z(from_above[low:], -1)])
    new_weight = jnp.zeros_like(weight)
    for step, rows in ((0, updated), (3, from_below), (1, from_above), (2, opposite)):
        for which_core, block in ((core, rows), (1 - core, to_other_core(rows))):
            shard = N_CORE * ((z_hi + step) % N_Z) + which_core
            new_weight = lax.dynamic_update_slice_in_dim(
                new_weight, block, shard * shard_rows, 0
            )
    return (new_weight, new_first[None], new_second[None])


def solution(mesh):
    placed = (
        P(("dp", "section"), "mp"),
        P("mp", "section"),
        P("dp", "section"),
        P("dp"),
        P("dp"),
        P("dp"),
        P(),
        P(),
        P(),
        P("mp", "dp", "section"),
        P("mp", "dp", "section"),
    )
    return jax.shard_map(
        on_device,
        mesh=mesh,
        in_specs=placed,
        out_specs=(P("mp", "section"), P("mp", "dp", "section"), P("mp", "dp", "section")),
        check_vma=False,
    )
```

```python
import jax
import jax.numpy as jnp
from jax import lax
from jax.sharding import PartitionSpec as P

RESP_LEN = 384


clip_eps = 0.2
kl_coef = 0.1
beta_one = 0.9
beta_two = 0.95
adam_eps = 1e-08
learn_rate = 0.0003
weight_decay = 0.1
first_correct = 1.0 - 0.9**10
second_correct = 1.0 - 0.95**10


def token_terms(lengths, group_ids, rewards, positions, resp_len):
    total_resp = rewards.shape[0]
    members = (group_ids[:, None] == group_ids[None, :]).astype(jnp.float32)
    group_size = jnp.sum(members, axis=1)
    group_mean = jnp.sum(members * rewards[None, :], axis=1) / group_size
    deviation = rewards[None, :] - group_mean[:, None]
    group_spread = jnp.sqrt(jnp.sum(members * deviation * deviation, axis=1) / group_size)
    advantage = (rewards - group_mean) / jnp.maximum(group_spread, 1.0)
    response = positions // resp_len
    slot_index = (positions % resp_len).astype(jnp.float32)
    picker = (response[:, None] == jnp.arange(total_resp, dtype=jnp.int32)[None, :]).astype(
        jnp.float32
    )
    adv_token = jnp.sum(picker * advantage[None, :], axis=1)
    len_token = jnp.sum(picker * lengths.astype(jnp.float32)[None, :], axis=1)
    token_weight = jnp.where(slot_index < len_token, 1.0 / (len_token * total_resp), 0.0)
    return (adv_token, token_weight)


def token_loss(new_logp, old_logp, ref_logp, adv_token, token_weight):
    ratio = jnp.exp(new_logp - old_logp)
    surrogate = jnp.minimum(
        ratio * adv_token, jnp.clip(ratio, 1.0 - clip_eps, 1.0 + clip_eps) * adv_token
    )
    gap = ref_logp - new_logp
    kl_term = jnp.exp(gap) - gap - 1.0
    return jnp.sum(token_weight * (kl_coef * kl_term - surrogate))


def token_coeff(new_logp, old_logp, ref_logp, adv_token, token_weight):

    def loss_of(values):
        return token_loss(values, old_logp, ref_logp, adv_token, token_weight)

    _, pullback = jax.vjp(loss_of, new_logp)
    return pullback(jnp.float32(1.0))[0]


def adam_rows(weight_rows, first_rows, second_rows, gradient):
    new_first = beta_one * first_rows + (1.0 - beta_one) * gradient
    new_second = beta_two * second_rows + (1.0 - beta_two) * gradient * gradient
    current = weight_rows.astype(jnp.float32)
    update = (
        new_first / first_correct / (jnp.sqrt(new_second / second_correct) + adam_eps)
        + weight_decay * current
    )
    return ((current - learn_rate * update).astype(jnp.bfloat16), new_first, new_second)


def contract_rows(left, right):
    return lax.dot_general(
        left, right, (((0,), (0,)), ((), ())), preferred_element_type=jnp.float32
    )


N_SEC = 8
N_Z = 4
N_CORE = 2
N_X = 4
N_ZLO = 3


def along_section(value, step):
    return lax.ppermute(value, "section", [(i, (i + step) % N_SEC) for i in range(N_SEC)])


def along_z(value, step):
    pairs = [
        (N_CORE * z + c, N_CORE * ((z + step) % N_Z) + c) for z in range(N_Z) for c in range(N_CORE)
    ]
    return lax.ppermute(value, "dp", pairs)


def to_other_core(value):
    return lax.ppermute(value, "dp", [(i, i ^ 1) for i in range(N_Z * N_CORE)])


def turned(value, blocks):
    twice = jnp.concatenate([value, value], axis=0)
    return lax.dynamic_slice_in_dim(
        twice, blocks * (value.shape[0] // N_SEC), value.shape[0], 0
    )


def reduce_scores(share):
    copies = jnp.broadcast_to(share[None, :], (N_SEC * N_X * N_ZLO, share.shape[0]))
    shares = lax.all_to_all(copies, ("section", "mp"), 0, 0)
    return jnp.sum(shares, axis=0)


def along_z(value, step):
    pairs = [
        (N_CORE * z + c, N_CORE * ((z + step) % N_Z) + c) for z in range(N_Z) for c in range(N_CORE)
    ]
    return lax.ppermute(value, "dp", pairs)


def to_other_core(value):
    return lax.ppermute(value, "dp", [(i, i ^ 1) for i in range(N_Z * N_CORE)])


COLUMN_CUTS = (0, 384, 640)


def on_device(
    activations,
    weight,
    readout,
    logp_rest,
    old_logp,
    ref_logp,
    lengths,
    group_ids,
    rewards,
    first_moment,
    second_moment,
):
    tok_block = activations.shape[0]
    tok_rep = tok_block * N_SEC
    section = lax.axis_index("section")
    dp = lax.axis_index("dp")
    core = dp % N_CORE
    z_hi = dp // N_CORE

    def own_first(value):
        return turned(value, section)

    readout = own_first(readout)

    def score_of(chunk, first_row):
        rows = lax.slice_in_dim(readout, first_row, first_row + chunk.shape[0], axis=0)
        product = jnp.dot(chunk, weight, preferred_element_type=jnp.float32)
        return jnp.sum(product * rows.astype(jnp.float32), axis=1)

    half = tok_block // 2
    pieces = [None] * (2 * N_SEC)
    scores = [None] * (2 * N_SEC)
    halves = [activations[:half], activations[half:]]
    below = list(halves)
    above = list(halves)
    pieces[0], pieces[1] = halves
    for step in range(1, N_SEC // 2):
        for part in range(2):
            below[part] = along_section(below[part], 1)
            above[part] = along_section(above[part], -1)
            pieces[2 * (N_SEC - step) + part] = below[part]
            pieces[2 * step + part] = above[part]
    pieces[N_SEC] = along_section(below[0], 1)
    pieces[N_SEC + 1] = along_section(above[1], -1)
    for j in range(2 * N_SEC):
        scores[j] = score_of(pieces[j], j * half)
    gathered = jnp.concatenate(pieces)
    share = turned(jnp.concatenate(scores), (N_SEC - section) % N_SEC)
    score = own_first(reduce_scores(share))

    lengths, group_ids, rewards, _ = lax.optimization_barrier((lengths, group_ids, rewards, share))
    new_logp = own_first(logp_rest) + score
    slots = jnp.arange(tok_rep, dtype=jnp.int32)
    positions = dp * tok_rep + (slots + section * tok_block) % tok_rep
    adv_token, token_weight = token_terms(lengths, group_ids, rewards, positions, RESP_LEN)
    coeff = token_coeff(
        new_logp, own_first(old_logp), own_first(ref_logp), adv_token, token_weight
    )
    shard_rows = first_moment.shape[1]
    low = shard_rows // 2
    lower, upper = slice(0, low), slice(low, shard_rows)

    chunks = [slice(a, b) for a, b in zip(COLUMN_CUTS[:-1], COLUMN_CUTS[1:])]
    parts, others = [], []
    for cols in chunks:
        weighted = (coeff[:, None] * readout[:, cols].astype(jnp.float32)).astype(jnp.bfloat16)
        part = contract_rows(gathered, weighted).astype(jnp.bfloat16)

        def part_rows(step, which_core, part=part):
            shard = N_CORE * ((z_hi + step) % N_Z) + which_core
            return lax.dynamic_slice_in_dim(part, shard * shard_rows, shard_rows, 0)

        parts.append([part_rows(step, core) for step in range(N_Z)])
        others.append(
            to_other_core(jnp.stack([part_rows(step, 1 - core) for step in range(N_Z)]))
        )

    def mine(chunk, step, rows):
        return parts[chunk][step][rows].astype(jnp.float32) + others[chunk][step][rows].astype(
            jnp.float32
        )

    n_chunks = len(chunks)
    up = [mine(k, 3, lower) for k in range(n_chunks)]
    down = [mine(k, 1, upper) for k in range(n_chunks)]
    for up_step, down_step in ((2, 2), (1, 3), (0, 0)):
        for k in range(n_chunks):
            up[k] = along_z(up[k].astype(jnp.bfloat16), 1).astype(jnp.float32)
            down[k] = along_z(down[k].astype(jnp.bfloat16), -1).astype(jnp.float32)
            up[k] = up[k] + mine(k, up_step, lower)
            down[k] = down[k] + mine(k, down_step, upper)

    weight_rows = lax.dynamic_slice_in_dim(weight, dp * shard_rows, shard_rows, 0)
    stepped = []
    for k, cols in enumerate(chunks):
        gradient = jnp.concatenate([up[k], down[k]])
        stepped.append(
            adam_rows(
                weight_rows[:, cols], first_moment[0][:, cols], second_moment[0][:, cols], gradient
            )
        )
    new_first = jnp.concatenate([part[1] for part in stepped], axis=1)
    new_second = jnp.concatenate([part[2] for part in stepped], axis=1)

    rows_of = []
    for updated, _, _ in stepped:
        rows_of.append({0: updated, 3: along_z(updated, 1), 1: along_z(updated, -1)})
    for blocks in rows_of:
        blocks[2] = jnp.concatenate([along_z(blocks[3][lower], 1), along_z(blocks[1][upper], -1)])
    new_weight = jnp.zeros_like(weight)
    for blocks, cols in zip(rows_of, chunks):
        near = to_other_core(jnp.stack([blocks[0], blocks[3], blocks[1]]))
        far = to_other_core(blocks[2])
        for step, passed in ((0, near[0]), (3, near[1]), (1, near[2]), (2, far)):
            for which_core, block in ((core, blocks[step]), (1 - core, passed)):
                shard = N_CORE * ((z_hi + step) % N_Z) + which_core
                new_weight = lax.dynamic_update_slice(
                    new_weight, block, (shard * shard_rows, cols.start)
                )
    return (new_weight, new_first[None], new_second[None])


def solution(mesh):
    placed = (
        P(("dp", "section"), "mp"),
        P("mp", "section"),
        P("dp", "section"),
        P("dp"),
        P("dp"),
        P("dp"),
        P(),
        P(),
        P(),
        P("mp", "dp", "section"),
        P("mp", "dp", "section"),
    )
    return jax.shard_map(
        on_device,
        mesh=mesh,
        in_specs=placed,
        out_specs=(P("mp", "section"), P("mp", "dp", "section"), P("mp", "dp", "section")),
        check_vma=False,
    )
```
